32 devices in a mesh: case: 4 (over z), gx: 2 (over y), gy: 4 (over x, core).
Axes of the slice: x: 2, y: 2, z: 4, core: 2. Of those that a mesh axis runs over, the one named last changes fastest.
Arguments:
- load: float32 [8, 24, 32, 128], P(('case', 'gx'), 'gy'), parts along dimension 0, may hold values from -4 to 4
- factors: bfloat16 [4, 8, 24, 128, 128], P(None, ('case', 'gx'), 'gy'), parts along dimension 1, may hold values from -6 to 6
- links: int32 [4, 8, 24], P(None, ('case', 'gx'), 'gy'), parts along dimension 1, may hold values from 0 to 1
- shift: float32 [8, 24, 128], P(('case', 'gx'), 'gy'), parts along dimension 0, may hold values from 0.25 to 2.5
Outputs:
- solution: float32 [8, 24, 32, 128], P(('case', 'gx'), 'gy'), parts along dimension 0
- residual: float32 [8, 24, 32, 128], P(('case', 'gx'), 'gy'), parts along dimension 0
The draws below stay inside these ranges and needn't reach their ends.
There are 4 independent parts, one for each index of `case`. The reference program is written for one: setup_inputs(seed, part) draws one part's arguments, and reference() takes and returns one part's arrays. A program takes and returns all parts, laid end to end along the dimension named above; each array names one. Nothing has to cross between parts.
All inputs are finite; a program needn't handle non-finite values.
Results may differ from the reference program's by a relative error of at most 0.008.
Values may be sent and summed in bfloat16 or wider, within the bound.
A program may use at most 64 MiB of HBM per device.

```python
import jax
import jax.numpy as jnp
from jax import lax

B = 128
NBX = 1
NBY = 6
NRHS = 32
ITERS = 8
NX = 2
NY = 24


OFFSETS = ((1, 0), (0, 1), (1, 1), (1, -1))


def displaced(array, step_x, step_y):
    padded = jnp.pad(array, ((1, 1), (1, 1)))
    return padded[1 + step_x:1 + step_x + NX, 1 + step_y:1 + step_y + NY]


def spike_plan(key):
    spike_key = jax.random.fold_in(key, 501)
    shards_x = NX // NBX
    shards_y = NY // NBY
    row_pick = jax.random.randint(jax.random.fold_in(spike_key, 1), (shards_x, shards_y), 0, NBX)
    column_pick = jax.random.randint(jax.random.fold_in(spike_key, 2), (shards_x, shards_y), 0, NBY - 1)
    active = jax.random.randint(jax.random.fold_in(spike_key, 3), (shards_x, shards_y), 0, 4)

    def expand(values):
        return jnp.repeat(jnp.repeat(values, NBX, axis=0), NBY, axis=1)
    local_x = jnp.arange(NX, dtype=jnp.int32) % NBX
    local_y = jnp.arange(NY, dtype=jnp.int32) % NBY
    chosen = (expand(active) > 0) & (local_x[:, None] == expand(row_pick)) & (local_y[None, :] == expand(column_pick))
    anchor = chosen.astype(jnp.int32)
    partner = displaced(anchor, 0, -1)
    marked = jnp.maximum(anchor, partner)
    return (anchor, marked)


def draw_load(key, part):
    sample = jax.random.normal(jax.random.fold_in(key, 11), (NX, NY, NRHS, B), jnp.float32)
    sample = jnp.clip(sample, -4.0, 4.0)
    return sample


def draw_links(key, part):
    anchor, marked = spike_plan(key)
    coupled = (jax.random.randint(jax.random.fold_in(key, 23), (4, NX, NY), 0, 4) > 0).astype(jnp.int32)
    touches = jnp.stack([jnp.maximum(marked, displaced(marked, step_x, step_y)) for step_x, step_y in OFFSETS])
    kept = coupled * (1 - touches)
    empty = jnp.zeros((NX, NY), jnp.int32)
    spiked = jnp.stack([empty, anchor, empty, empty])
    return jnp.maximum(kept, spiked).astype(jnp.int32)


def draw_factors(key, part):
    anchor, marked = spike_plan(key)
    noise = jax.random.normal(jax.random.fold_in(key, 37), (4, NX, NY, B, B), jnp.float32)
    noise = jnp.clip(noise, -6.0, 6.0)
    left = jax.random.randint(jax.random.fold_in(key, 43), (NX, NY, B), 0, 2).astype(jnp.float32) * 2.0 - 1.0
    right = jax.random.randint(jax.random.fold_in(key, 47), (NX, NY, B), 0, 2).astype(jnp.float32) * 2.0 - 1.0
    weight = 4.0 * anchor.astype(jnp.float32)[:, :, None, None]
    spike = weight * left[:, :, :, None] * right[:, :, None, :]
    noise = noise.at[1].add(spike)
    return jnp.clip(noise, -6.0, 6.0).astype(jnp.bfloat16)


def draw_shift(key, part):
    anchor, marked = spike_plan(key)
    values = jax.random.uniform(jax.random.fold_in(key, 41), (NX, NY, B), jnp.float32, 0.25, 2.5)
    return jnp.where(marked[:, :, None] > 0, 0.5, values).astype(jnp.float32)


def setup_inputs(seed: int = 0, part: int = 0) -> dict:
    arg_keys = jax.random.split(jax.random.key(seed), 5)
    own_keys = jax.random.split(jax.random.fold_in(arg_keys[4], part), 5)
    return {
        "load": draw_load(jax.random.fold_in(jax.random.fold_in(arg_keys[4], part), 71), part),
        "factors": draw_factors(jax.random.fold_in(jax.random.fold_in(arg_keys[4], part), 71), part),
        "links": draw_links(jax.random.fold_in(jax.random.fold_in(arg_keys[4], part), 71), part),
        "shift": draw_shift(jax.random.fold_in(jax.random.fold_in(arg_keys[4], part), 71), part),
    }


OFFSETS = ((1, 0), (0, 1), (1, 1), (1, -1))
PRECISE = lax.Precision.HIGHEST

def neighbour(array, step_x, step_y):
    count_x, count_y = (array.shape[0], array.shape[1])
    widths = ((1, 1), (1, 1)) + ((0, 0),) * (array.ndim - 2)
    padded = jnp.pad(array, widths)
    return padded[1 + step_x:1 + step_x + count_x, 1 + step_y:1 + step_y + count_y]

def apply_block(block, field):
    return jnp.einsum('xyab,xyrb->xyra', block.astype(jnp.float32), field.astype(jnp.float32), precision=PRECISE, preferred_element_type=jnp.float32)

def inner(left, right):
    return jnp.sum(left * right, axis=(0, 1, 3))

def spread(values):
    return values[None, None, :, None]

def reference(load, factors, links, shift):
    masked = factors.astype(jnp.float32) * links.astype(jnp.float32)[:, :, :, None, None]
    springs = jnp.einsum('dxyak,dxybk->dxyab', masked.astype(jnp.float32), masked.astype(jnp.float32), precision=PRECISE, preferred_element_type=jnp.float32) / B
    forward = [springs[offset] for offset in range(4)]
    backward = [neighbour(springs[offset], -OFFSETS[offset][0], -OFFSETS[offset][1]) for offset in range(4)]
    identity = jnp.eye(B, dtype=jnp.float32)
    diagonal = shift[..., None] * identity + sum(forward) + sum(backward)
    flat = diagonal.reshape(-1, B, B)
    lower = jnp.linalg.cholesky(flat)
    inverse = jax.vmap(lambda factor: jax.scipy.linalg.cho_solve((factor, True), identity))(lower).reshape(diagonal.shape)

    def operate(field):
        result = apply_block(diagonal, field)
        for offset in range(4):
            step_x, step_y = OFFSETS[offset]
            result = result - apply_block(forward[offset], neighbour(field, step_x, step_y))
            result = result - apply_block(backward[offset], neighbour(field, -step_x, -step_y))
        return result
    solution = jnp.zeros_like(load)
    residual = load
    precon = apply_block(inverse, residual)
    direction = precon
    rz_now = inner(residual, precon)
    for iteration in range(ITERS):
        image = operate(direction)
        alpha = rz_now / inner(direction, image)
        solution = solution + spread(alpha) * direction
        residual = residual - spread(alpha) * image
        precon = apply_block(inverse, residual)
        rz_next = inner(residual, precon)
        direction = precon + spread(rz_next / rz_now) * direction
        rz_now = rz_next
    return (solution, residual)
```

```python
import functools

import jax
import jax.numpy as jnp
from jax import lax
from jax.experimental import pallas as pl
from jax.experimental.pallas import tpu as pltpu
from jax.sharding import PartitionSpec as P

B = 128
ITERS = 8


OFFSETS = ((1, 0), (0, 1), (1, 1), (1, -1))
PRECISE = lax.Precision.HIGHEST


def extended(cells, sides, width):
    for axis, dim in sides:
        count = lax.axis_size(axis)
        ends = count - 1
        head = lax.slice_in_dim(cells, 0, width, axis=dim)
        tail = lax.slice_in_dim(cells, cells.shape[dim] - width, cells.shape[dim], axis=dim)
        cells = jnp.concatenate(
            [
                lax.ppermute(tail, axis, [(i, (i + 1) % count) for i in range(ends)]),
                cells,
                lax.ppermute(head, axis, [((i + 1) % count, i) for i in range(ends)]),
            ],
            axis=dim,
        )
    return cells


def window(padded, step_x, step_y, count_x, count_y):
    return padded[1 + step_x : 1 + step_x + count_x, 1 + step_y : 1 + step_y + count_y]


def inner(left, right):
    return jnp.sum(left * right, axis=(0, 1, 3))


def spread(values):
    return values[None, None, :, None]


def local(load, factors, links, shift):
    count_x, count_y = (load.shape[0], load.shape[1])
    masked = factors * links.astype(jnp.bfloat16)[:, :, :, None, None]
    springs = (
        jnp.einsum("dxyak,dxybk->dxyab", masked, masked, preferred_element_type=jnp.float32) / B
    )
    padded_springs = extended(springs, (("gx", 1), ("gy", 2)), 1)
    forward = padded_springs[:, 1:-1, 1:-1]
    backward = jnp.stack(
        [
            window(
                padded_springs[offset], -OFFSETS[offset][0], -OFFSETS[offset][1], count_x, count_y
            )
            for offset in range(4)
        ]
    )
    identity = jnp.eye(B, dtype=jnp.float32)
    diagonal = shift[..., None] * identity + jnp.sum(forward, axis=0) + jnp.sum(backward, axis=0)
    lower = jnp.linalg.cholesky(diagonal.reshape(-1, B, B))
    inverse = jax.vmap(lambda factor: jax.scipy.linalg.cho_solve((factor, True), identity))(
        lower
    ).reshape(diagonal.shape)
    blocks = jnp.concatenate([diagonal[None], -forward, -backward], axis=0)

    def operate(field):
        padded = extended(field, (("gx", 0), ("gy", 1)), 1)
        pieces = [field]
        pieces = pieces + [
            window(padded, step_x, step_y, count_x, count_y) for step_x, step_y in OFFSETS
        ]
        pieces = pieces + [
            window(padded, -step_x, -step_y, count_x, count_y) for step_x, step_y in OFFSETS
        ]
        return jnp.einsum(
            "kxyab,kxyrb->xyra",
            blocks,
            jnp.stack(pieces),
            precision=PRECISE,
            preferred_element_type=jnp.float32,
        )

    def precondition(field):
        return jnp.einsum(
            "xyab,xyrb->xyra", inverse, field, precision=PRECISE, preferred_element_type=jnp.float32
        )

    def paired(residual, precon, image):
        return lax.psum((inner(residual, precon), inner(image, precon)), ("gx", "gy"))

    solution = jnp.zeros_like(load)
    residual = load
    precon = precondition(residual)
    image = operate(precon)
    gamma, delta = paired(residual, precon, image)
    alpha = gamma / delta
    direction, along = (precon, image)
    for iteration in range(ITERS):
        solution = solution + spread(alpha) * direction
        residual = residual - spread(alpha) * along
        if iteration + 1 < ITERS:
            precon = precondition(residual)
            image = operate(precon)
            gamma_next, delta = paired(residual, precon, image)
            ratio = gamma_next / gamma
            alpha = gamma_next / (delta - ratio * gamma_next / alpha)
            direction = precon + spread(ratio) * direction
            along = image + spread(ratio) * along
            gamma = gamma_next
    return (solution, residual)


F32 = jnp.float32
BF16 = jnp.bfloat16
PANEL = 8


def split3(value):
    high = value.astype(BF16)
    rest = value - high.astype(F32)
    mid = rest.astype(BF16)
    low = (rest - mid.astype(F32)).astype(BF16)
    return high, mid, low


def fused(gy_count, load_ref, fac_ref, links_ref, shift_ref, x_out, r_out,
          fac, out_fac, hal_fac, sh, out_sh, spr, dia, wa, wb,
          xs, rs, ps, ss, zs, hv, red, ret,
          fac_sem, half_sem, hal_sem, v_sem, red_sem, ret_sem):
    g = lax.axis_index("gx")
    k = lax.axis_index("gy")
    n = 2 * gy_count
    p = 2 * k + g
    nc = fac.shape[2]
    nr = load_ref.shape[2]
    other = 1 - g
    mesh_id = pl.DeviceIdType.MESH

    def at(gx, gy):
        return {"gx": gx, "gy": gy}

    partner = at(other, k)
    left = at(other, k - other)
    right = at(other, k + g)

    barrier = pltpu.get_barrier_semaphore()
    peers = []
    for q in range(1, n):
        t = lax.rem(p + q, n)
        peers.append(at(lax.rem(t, 2), t // 2))
    for peer in peers:
        pl.semaphore_signal(barrier, inc=1, device_id=peer, device_id_type=mesh_id)

    def remote(src, dst, sems, peer):
        return pltpu.make_async_remote_copy(
            src_ref=src, dst_ref=dst, send_sem=sems.at[0], recv_sem=sems.at[1],
            device_id=peer, device_id_type=mesh_id)

    for j in range(nc):
        out_sh[j] = jnp.broadcast_to(shift_ref[0, pl.ds(other * nc + j, 1), :], (8, B))
        sh[g, j] = jnp.broadcast_to(shift_ref[0, pl.ds(g * nc + j, 1), :], (8, B))
        for d in range(4):
            here, there = g * nc + j, other * nc + j
            out_fac[d, j] = (fac_ref[d, 0, there].astype(F32) * links_ref[d, 0, there].astype(F32)).astype(BF16)
            fac[d, g, j] = (fac_ref[d, 0, here].astype(F32) * links_ref[d, 0, here].astype(F32)).astype(BF16)
        rs[g, j] = load_ref[0, g * nc + j]

    @pl.when(p == 0)
    def _():
        hal_fac[0:3] = jnp.zeros((3, B, B), BF16)
        hv[:, 0] = jnp.zeros(hv.shape[:1] + hv.shape[2:], F32)

    @pl.when(p == n - 1)
    def _():
        hal_fac[3] = jnp.zeros((B, B), BF16)
        hv[:, 1] = jnp.zeros(hv.shape[:1] + hv.shape[2:], F32)

    pl.semaphore_wait(barrier, n - 1)

    halves = [remote(out_fac.at[d], fac.at[d, g], fac_sem.at[d], partner) for d in (1, 2, 3, 0)]
    halves.append(remote(out_sh, sh.at[g], half_sem.at[0], partner))
    halves.append(remote(load_ref.at[0, pl.ds(other * nc, nc)], rs.at[g], half_sem.at[1], partner))
    for copy in halves:
        copy.start()

    def spring(f):
        return lax.dot_general(f, f, (((1,), (1,)), ((), ())), preferred_element_type=F32) * (1.0 / B)

    for d in range(4):
        for j in range(nc):
            spr[d, g, j] = spring(fac[d, g, j])
    for copy in halves:
        copy.wait()

    sides = [
        (remote(fac.at[1, 0, nc - 1], hal_fac.at[0], hal_sem.at[0], right), True),
        (remote(fac.at[1, 1, nc - 1], hal_fac.at[1], hal_sem.at[1], right), True),
        (remote(fac.at[2, 0, nc - 1], hal_fac.at[2], hal_sem.at[2], right), True),
        (remote(fac.at[3, 0, 0], hal_fac.at[3], hal_sem.at[3], left), False),
    ]

    @pl.when(p < n - 1)
    def _():
        for copy, rightward in sides:
            if rightward:
                copy.start()

    @pl.when(p > 0)
    def _():
        for copy, rightward in sides:
            if not rightward:
                copy.start()

    for d in range(4):
        for j in range(nc):
            spr[d, other, j] = spring(fac[d, other, j])

    @pl.when(p < n - 1)
    def _():
        for copy, rightward in sides:
            if rightward:
                copy.wait_send()
            else:
                copy.wait_recv()

    @pl.when(p > 0)
    def _():
        for copy, rightward in sides:
            if rightward:
                copy.wait_recv()
            else:
                copy.wait_send()

    def keep(i, value):
        high, mid, low = split3(value)
        wa[i, 0:B] = high
        wa[i, B:2 * B] = mid
        wb[i] = low

    i0, i1, i2, i3, il = 0, nc, 3 * nc, 4 * nc, 5 * nc
    ih = 6 * nc
    im = ih + 4
    for s in range(4):
        keep(ih + s, spring(hal_fac[s]))
    back = [spring(hal_fac[s]) for s in range(4)]
    eye = (lax.broadcasted_iota(jnp.int32, (B, B), 0) == lax.broadcasted_iota(jnp.int32, (B, B), 1)).astype(F32)
    for j in range(nc):
        keep(i0 + j, spr[0, 0, j])
        keep(i1 + j, spr[1, 0, j])
        keep(i1 + nc + j, spr[1, 1, j])
        keep(i2 + j, spr[2, 0, j])
        keep(i3 + j, spr[3, 0, j])
        edge = spr[0, 1, j] + spr[2, 1, j] + spr[3, 1, j]
        keep(il + j, edge)
        before0 = back[0] if j == 0 else spr[1, 0, j - 1]
        before1 = back[1] if j == 0 else spr[1, 1, j - 1]
        upper = spr[0, 0, j] + spr[1, 0, j] + spr[2, 0, j] + spr[3, 0, j] + before0
        lower = edge + spr[1, 1, j] + before1 + spr[0, 0, j]
        lower = lower + (back[2] if j == 0 else spr[2, 0, j - 1])
        lower = lower + (back[3] if j == nc - 1 else spr[3, 0, j + 1])
        dia[j] = upper + eye * sh[0, j, 0:1, :]
        dia[nc + j] = lower + eye * sh[1, j, 0:1, :]

    count = 2 * nc
    lane = lax.broadcasted_iota(jnp.int32, (1, PANEL, B), 2)
    row = lax.broadcasted_iota(jnp.int32, (1, PANEL, B), 1)
    big_lane = lax.broadcasted_iota(jnp.int32, (B, B), 1)
    big_row = lax.broadcasted_iota(jnp.int32, (B, B), 0)

    def parts(value):
        high = value.astype(BF16).astype(F32)
        rest = value - high
        mid = rest.astype(BF16).astype(F32)
        return high, mid, rest - mid

    def sweep(step, carry):
        first = pl.multiple_of(step * PANEL, PANEL)
        panel = dia[:, pl.ds(first, PANEL), :]
        across = jnp.where(lane < first, -panel, panel)
        inside = (lane >= first) & (lane < first + PANEL)
        across = jnp.where(inside, jnp.where(lane == row + first, -1.0, 0.0), across)
        flat = pltpu.roll(panel.reshape(count * PANEL, B), lax.rem(B - first, B), 1)
        turned = flat.reshape(count, PANEL, B)
        for j in range(PANEL):
            inv = 1.0 / turned[:, j:j + 1, j:j + 1]
            line = jnp.where(lane == j, inv, turned[:, j:j + 1, :] * inv)
            column = turned[:, :, j:j + 1]
            turned = jnp.where(row == j, line, jnp.where(lane == j, 0.0, turned) - column * line)
        solved = pltpu.roll(turned.reshape(count * PANEL, B), first, 1).reshape(count, PANEL, B)
        hidden = ((big_lane >= first) & (big_lane < first + PANEL)) | (
            (big_row >= first) & (big_row < first + PANEL))
        for m in range(count):
            ah, am, al = parts(across[m])
            bh, bm, bl = parts(solved[m])
            lhs = jnp.concatenate([ah, ah, ah, am, am, al], axis=0).astype(BF16)
            rhs = jnp.concatenate([bh, bm, bl, bh, bm, bh], axis=0).astype(BF16)
            product = lax.dot_general(lhs, rhs, (((0,), (0,)), ((), ())), preferred_element_type=F32)
            dia[m] = jnp.where(hidden, 0.0, dia[m]) - product
        return carry

    lax.fori_loop(0, B // PANEL, sweep, 0)
    for m in range(count):
        keep(im + m, dia[m])

    def times(value, i):
        high, mid, low = split3(value)
        stacked = jnp.concatenate([
            jnp.concatenate([high, high], axis=1),
            jnp.concatenate([mid, mid], axis=1),
            jnp.concatenate([low, low], axis=1)], axis=0)
        out = jnp.dot(stacked, wa[i], preferred_element_type=F32)
        tail = jnp.dot(high, wb[i], preferred_element_type=F32)
        return out[0:nr] + (out[nr:2 * nr] + (out[2 * nr:3 * nr] + tail))

    xs[...] = jnp.zeros_like(xs)
    ps[...] = jnp.zeros_like(ps)
    ss[...] = jnp.zeros_like(ss)
    vlane = lax.broadcasted_iota(jnp.int32, (nr, B), 1)
    vrow = lax.broadcasted_iota(jnp.int32, (nr, B), 0)

    def iterate(t, carry):
        gamma_old, alpha_old = carry
        z = [[times(rs[x, j], im + x * nc + j) for j in range(nc)] for x in range(2)]
        for x in range(2):
            zs[t, 0, x] = z[x][0]
            zs[t, 1, x] = z[x][nc - 1]
        to_left = remote(zs.at[t, 0], hv.at[t, 1], v_sem.at[t, 0], left)
        to_right = remote(zs.at[t, 1], hv.at[t, 0], v_sem.at[t, 1], right)

        @pl.when(p > 0)
        def _():
            to_left.start()

        @pl.when(p < n - 1)
        def _():
            to_right.start()

        w = [[z[x][j] * sh[x, j, 0:1, :] for j in range(nc)] for x in range(2)]
        for j in range(nc):
            w[1][j] = w[1][j] + times(z[1][j], il + j)
            flux = times(z[0][j] - z[1][j], i0 + j)
            w[0][j] = w[0][j] + flux
            w[1][j] = w[1][j] - flux
            if j + 1 < nc:
                for x in range(2):
                    flux = times(z[x][j] - z[x][j + 1], i1 + x * nc + j)
                    w[x][j] = w[x][j] + flux
                    w[x][j + 1] = w[x][j + 1] - flux
                flux = times(z[0][j] - z[1][j + 1], i2 + j)
                w[0][j] = w[0][j] + flux
                w[1][j + 1] = w[1][j + 1] - flux
            if j > 0:
                flux = times(z[0][j] - z[1][j - 1], i3 + j)
                w[0][j] = w[0][j] + flux
                w[1][j - 1] = w[1][j - 1] - flux

        @pl.when(p > 0)
        def _():
            to_right.wait_recv()
            to_left.wait_send()

        @pl.when(p < n - 1)
        def _():
            to_left.wait_recv()
            to_right.wait_send()

        e = nc - 1
        from_left = [hv[t, 0, x] for x in range(2)]
        from_right = [hv[t, 1, x] for x in range(2)]
        for x in range(2):
            w[x][e] = w[x][e] + times(z[x][e] - from_right[x], i1 + x * nc + e)
            w[x][0] = w[x][0] - times(from_left[x] - z[x][0], ih + x)
        w[0][e] = w[0][e] + times(z[0][e] - from_right[1], i2 + e)
        w[1][0] = w[1][0] - times(from_left[0] - z[1][0], ih + 2)
        w[0][0] = w[0][0] + times(z[0][0] - from_left[1], i3)
        w[1][e] = w[1][e] - times(from_right[0] - z[1][e], ih + 3)

        dot_rz = jnp.zeros((nr, B), F32)
        dot_wz = jnp.zeros((nr, B), F32)
        for x in range(2):
            for j in range(nc):
                dot_rz = dot_rz + rs[x, j] * z[x][j]
                dot_wz = dot_wz + w[x][j] * z[x][j]
        mine = jnp.where(vlane == vrow, jnp.sum(dot_rz, axis=1, keepdims=True), 0.0)
        mine = mine + jnp.where(vlane == vrow + nr, jnp.sum(dot_wz, axis=1, keepdims=True), 0.0)
        packed = mine[0:8]
        for q in range(8, nr, 8):
            packed = packed + mine[q:q + 8]
        red[t, p] = packed
        sends = [remote(red.at[t, p], red.at[t, p], red_sem.at[t, q], peer) for q, peer in enumerate(peers)]
        for copy in sends:
            copy.start()
        for copy in sends:
            copy.wait()
        total = red[t, 0]
        for q in range(1, n):
            total = total + red[t, q]
        total = jnp.concatenate([total] * (nr // 8), axis=0)
        gamma = jnp.sum(jnp.where(vlane == vrow, total, 0.0), axis=1, keepdims=True)
        delta = jnp.sum(jnp.where(vlane == vrow + nr, total, 0.0), axis=1, keepdims=True)
        start = t == 0
        ratio = jnp.where(start, 0.0, gamma / gamma_old)
        alpha = gamma / jnp.where(start, delta, delta - ratio * gamma / alpha_old)
        for x in range(2):
            for j in range(nc):
                direction = z[x][j] + ratio * ps[x, j]
                along = w[x][j] + ratio * ss[x, j]
                ps[x, j] = direction
                ss[x, j] = along
                xs[x, j] = xs[x, j] + alpha * direction
                rs[x, j] = rs[x, j] - alpha * along
        return gamma, alpha

    one = jnp.ones((nr, 1), F32)
    lax.fori_loop(0, ITERS, iterate, (one, one))

    homes = [
        remote(xs.at[other], ret.at[0], ret_sem.at[0], partner),
        remote(rs.at[other], ret.at[1], ret_sem.at[1], partner),
    ]
    for copy in homes:
        copy.start()
    for j in range(nc):
        x_out[0, g * nc + j] = xs[g, j]
        r_out[0, g * nc + j] = rs[g, j]
    for copy in homes:
        copy.wait()
    for j in range(nc):
        x_out[0, other * nc + j] = ret[0, j]
        r_out[0, other * nc + j] = ret[1, j]


def paired_rows(gy_count):
    def run(load, factors, links, shift):
        nc = load.shape[1] // 2
        nr = load.shape[2]
        n = 2 * gy_count
        blocks = 6 * nc + 4 + 2 * nc
        dma = pltpu.SemaphoreType.DMA
        vmem = pltpu.VMEM
        node = (2, nc, nr, B)
        return pl.pallas_call(
            functools.partial(fused, gy_count),
            out_shape=[jax.ShapeDtypeStruct(load.shape, F32)] * 2,
            in_specs=[
                pl.BlockSpec(memory_space=vmem),
                pl.BlockSpec(memory_space=vmem),
                pl.BlockSpec(memory_space=pltpu.SMEM),
                pl.BlockSpec(memory_space=vmem),
            ],
            out_specs=[pl.BlockSpec(memory_space=vmem)] * 2,
            scratch_shapes=[
                vmem((4, 2, nc, B, B), BF16),
                vmem((4, nc, B, B), BF16),
                vmem((4, B, B), BF16),
                vmem((2, nc, 8, B), F32),
                vmem((nc, 8, B), F32),
                vmem((4, 2, nc, B, B), F32),
                vmem((2 * nc, B, B), F32),
                vmem((blocks, 2 * B, B), BF16),
                vmem((blocks, B, B), BF16),
                vmem(node, F32),
                vmem(node, F32),
                vmem(node, F32),
                vmem(node, F32),
                vmem((ITERS, 2, 2, nr, B), F32),
                vmem((ITERS, 2, 2, nr, B), F32),
                vmem((ITERS, n, 8, B), F32),
                vmem((2, nc, nr, B), F32),
                dma((4, 2)),
                dma((2, 2)),
                dma((4, 2)),
                dma((ITERS, 2, 2)),
                dma((ITERS, n - 1, 2)),
                dma((2, 2)),
            ],
            compiler_params=pltpu.CompilerParams(
                collective_id=0, has_side_effects=True, vmem_limit_bytes=48 * 1024 * 1024),
        )(load, factors, links, shift)

    return run


def solution(mesh):
    placed = (
        P(("case", "gx"), "gy", None, None),
        P(None, ("case", "gx"), "gy", None, None),
        P(None, ("case", "gx"), "gy"),
        P(("case", "gx"), "gy", None),
    )
    paired_grid = mesh.shape["gx"] == 2
    return jax.shard_map(
        paired_rows(mesh.shape["gy"]) if paired_grid else local,
        mesh=mesh,
        in_specs=placed,
        out_specs=(P(("case", "gx"), "gy", None, None), P(("case", "gx"), "gy", None, None)),
        check_vma=False,
    )
```

```python
import functools

import jax
import jax.numpy as jnp
from jax import lax
from jax.experimental import pallas as pl
from jax.experimental.pallas import tpu as pltpu
from jax.sharding import PartitionSpec as P

B = 128
ITERS = 8


OFFSETS = ((1, 0), (0, 1), (1, 1), (1, -1))
PRECISE = lax.Precision.HIGHEST


def extended(cells, sides, width):
    for axis, dim in sides:
        count = lax.axis_size(axis)
        ends = count - 1
        head = lax.slice_in_dim(cells, 0, width, axis=dim)
        tail = lax.slice_in_dim(cells, cells.shape[dim] - width, cells.shape[dim], axis=dim)
        cells = jnp.concatenate(
            [
                lax.ppermute(tail, axis, [(i, (i + 1) % count) for i in range(ends)]),
                cells,
                lax.ppermute(head, axis, [((i + 1) % count, i) for i in range(ends)]),
            ],
            axis=dim,
        )
    return cells


def window(padded, step_x, step_y, count_x, count_y):
    return padded[1 + step_x : 1 + step_x + count_x, 1 + step_y : 1 + step_y + count_y]


def inner(left, right):
    return jnp.sum(left * right, axis=(0, 1, 3))


def spread(values):
    return values[None, None, :, None]


def local(load, factors, links, shift):
    count_x, count_y = (load.shape[0], load.shape[1])
    masked = factors * links.astype(jnp.bfloat16)[:, :, :, None, None]
    springs = (
        jnp.einsum("dxyak,dxybk->dxyab", masked, masked, preferred_element_type=jnp.float32) / B
    )
    padded_springs = extended(springs, (("gx", 1), ("gy", 2)), 1)
    forward = padded_springs[:, 1:-1, 1:-1]
    backward = jnp.stack(
        [
            window(
                padded_springs[offset], -OFFSETS[offset][0], -OFFSETS[offset][1], count_x, count_y
            )
            for offset in range(4)
        ]
    )
    identity = jnp.eye(B, dtype=jnp.float32)
    diagonal = shift[..., None] * identity + jnp.sum(forward, axis=0) + jnp.sum(backward, axis=0)
    lower = jnp.linalg.cholesky(diagonal.reshape(-1, B, B))
    inverse = jax.vmap(lambda factor: jax.scipy.linalg.cho_solve((factor, True), identity))(
        lower
    ).reshape(diagonal.shape)
    blocks = jnp.concatenate([diagonal[None], -forward, -backward], axis=0)

    def operate(field):
        padded = extended(field, (("gx", 0), ("gy", 1)), 1)
        pieces = [field]
        pieces = pieces + [
            window(padded, step_x, step_y, count_x, count_y) for step_x, step_y in OFFSETS
        ]
        pieces = pieces + [
            window(padded, -step_x, -step_y, count_x, count_y) for step_x, step_y in OFFSETS
        ]
        return jnp.einsum(
            "kxyab,kxyrb->xyra",
            blocks,
            jnp.stack(pieces),
            precision=PRECISE,
            preferred_element_type=jnp.float32,
        )

    def precondition(field):
        return jnp.einsum(
            "xyab,xyrb->xyra", inverse, field, precision=PRECISE, preferred_element_type=jnp.float32
        )

    def paired(residual, precon, image):
        return lax.psum((inner(residual, precon), inner(image, precon)), ("gx", "gy"))

    solution = jnp.zeros_like(load)
    residual = load
    precon = precondition(residual)
    image = operate(precon)
    gamma, delta = paired(residual, precon, image)
    alpha = gamma / delta
    direction, along = (precon, image)
    for iteration in range(ITERS):
        solution = solution + spread(alpha) * direction
        residual = residual - spread(alpha) * along
        if iteration + 1 < ITERS:
            precon = precondition(residual)
            image = operate(precon)
            gamma_next, delta = paired(residual, precon, image)
            ratio = gamma_next / gamma
            alpha = gamma_next / (delta - ratio * gamma_next / alpha)
            direction = precon + spread(ratio) * direction
            along = image + spread(ratio) * along
            gamma = gamma_next
    return (solution, residual)


F32 = jnp.float32
BF16 = jnp.bfloat16
PANEL = 8


def split3(value):
    high = value.astype(BF16)
    rest = value - high.astype(F32)
    mid = rest.astype(BF16)
    low = (rest - mid.astype(F32)).astype(BF16)
    return high, mid, low


def fused(gy_count, load_ref, fac_ref, links_ref, shift_ref, x_out, r_out,
          fac, out_fac, hal_fac, sh, out_sh, spr, dia, wa, wb,
          xs, rs, ps, ss, ws, hv, mrim, rrim, srim, red, ret,
          fac_sem, half_sem, hal_sem, m_sem, r_sem, v_sem, red_sem, ret_sem):
    g = lax.axis_index("gx")
    k = lax.axis_index("gy")
    n = 2 * gy_count
    p = 2 * k + g
    nc = fac.shape[2]
    nr = load_ref.shape[2]
    other = 1 - g
    mesh_id = pl.DeviceIdType.MESH

    def at(gx, gy):
        return {"gx": gx, "gy": gy}

    partner = at(other, k)
    left = at(other, k - other)
    right = at(other, k + g)

    barrier = pltpu.get_barrier_semaphore()
    peers = []
    for q in range(1, n):
        t = lax.rem(p + q, n)
        peers.append(at(lax.rem(t, 2), t // 2))
    for peer in peers:
        pl.semaphore_signal(barrier, inc=1, device_id=peer, device_id_type=mesh_id)

    def remote(src, dst, sems, peer):
        return pltpu.make_async_remote_copy(
            src_ref=src, dst_ref=dst, send_sem=sems.at[0], recv_sem=sems.at[1],
            device_id=peer, device_id_type=mesh_id)

    def start_edges(copies):
        @pl.when(p < n - 1)
        def _():
            for copy, rightward in copies:
                if rightward:
                    copy.start()

        @pl.when(p > 0)
        def _():
            for copy, rightward in copies:
                if not rightward:
                    copy.start()

    def wait_edges(copies):
        @pl.when(p < n - 1)
        def _():
            for copy, rightward in copies:
                if rightward:
                    copy.wait_send()
                else:
                    copy.wait_recv()

        @pl.when(p > 0)
        def _():
            for copy, rightward in copies:
                if rightward:
                    copy.wait_recv()
                else:
                    copy.wait_send()

    for j in range(nc):
        out_sh[j] = jnp.broadcast_to(shift_ref[0, pl.ds(other * nc + j, 1), :], (8, B))
        sh[g, j] = jnp.broadcast_to(shift_ref[0, pl.ds(g * nc + j, 1), :], (8, B))
        for d in range(4):
            here, there = g * nc + j, other * nc + j
            out_fac[d, j] = (fac_ref[d, 0, there].astype(F32) * links_ref[d, 0, there].astype(F32)).astype(BF16)
            fac[d, g, j] = (fac_ref[d, 0, here].astype(F32) * links_ref[d, 0, here].astype(F32)).astype(BF16)
        rs[g, j] = load_ref[0, g * nc + j]

    @pl.when(p == 0)
    def _():
        hal_fac[0:3] = jnp.zeros((3, B, B), BF16)
        hv[:, 0] = jnp.zeros(hv.shape[:1] + hv.shape[2:], F32)
        mrim[0] = jnp.zeros(mrim.shape[1:], F32)
        rrim[0] = jnp.zeros(rrim.shape[1:], F32)

    @pl.when(p == n - 1)
    def _():
        hal_fac[3] = jnp.zeros((B, B), BF16)
        hv[:, 1] = jnp.zeros(hv.shape[:1] + hv.shape[2:], F32)
        mrim[1] = jnp.zeros(mrim.shape[1:], F32)
        rrim[1] = jnp.zeros(rrim.shape[1:], F32)

    pl.semaphore_wait(barrier, n - 1)

    halves = [remote(out_fac.at[d], fac.at[d, g], fac_sem.at[d], partner) for d in (1, 2, 3, 0)]
    halves.append(remote(out_sh, sh.at[g], half_sem.at[0], partner))
    halves.append(remote(load_ref.at[0, pl.ds(other * nc, nc)], rs.at[g], half_sem.at[1], partner))
    for copy in halves:
        copy.start()

    def spring(f):
        return lax.dot_general(f, f, (((1,), (1,)), ((), ())), preferred_element_type=F32) * (1.0 / B)

    for d in range(4):
        for j in range(nc):
            spr[d, g, j] = spring(fac[d, g, j])
    for copy in halves:
        copy.wait()

    sides = [
        (remote(fac.at[1, 0, nc - 1], hal_fac.at[0], hal_sem.at[0], right), True),
        (remote(fac.at[1, 1, nc - 1], hal_fac.at[1], hal_sem.at[1], right), True),
        (remote(fac.at[2, 0, nc - 1], hal_fac.at[2], hal_sem.at[2], right), True),
        (remote(fac.at[3, 0, 0], hal_fac.at[3], hal_sem.at[3], left), False),
        (remote(rs.at[:, nc - 1], rrim.at[0], r_sem.at[0], right), True),
        (remote(rs.at[:, 0], rrim.at[1], r_sem.at[1], left), False),
    ]

    start_edges(sides)

    for d in range(4):
        for j in range(nc):
            spr[d, other, j] = spring(fac[d, other, j])

    wait_edges(sides)

    def keep(i, value):
        high, mid, low = split3(value)
        wa[i, 0:B] = high
        wa[i, B:2 * B] = mid
        wb[i] = low

    i0, i1, i2, i3, il = 0, nc, 3 * nc, 4 * nc, 5 * nc
    ih = 6 * nc
    im = ih + 4
    for s in range(4):
        keep(ih + s, spring(hal_fac[s]))
    back = [spring(hal_fac[s]) for s in range(4)]
    eye = (lax.broadcasted_iota(jnp.int32, (B, B), 0) == lax.broadcasted_iota(jnp.int32, (B, B), 1)).astype(F32)
    for j in range(nc):
        keep(i0 + j, spr[0, 0, j])
        keep(i1 + j, spr[1, 0, j])
        keep(i1 + nc + j, spr[1, 1, j])
        keep(i2 + j, spr[2, 0, j])
        keep(i3 + j, spr[3, 0, j])
        edge = spr[0, 1, j] + spr[2, 1, j] + spr[3, 1, j]
        keep(il + j, edge)
        before0 = back[0] if j == 0 else spr[1, 0, j - 1]
        before1 = back[1] if j == 0 else spr[1, 1, j - 1]
        upper = spr[0, 0, j] + spr[1, 0, j] + spr[2, 0, j] + spr[3, 0, j] + before0
        lower = edge + spr[1, 1, j] + before1 + spr[0, 0, j]
        lower = lower + (back[2] if j == 0 else spr[2, 0, j - 1])
        lower = lower + (back[3] if j == nc - 1 else spr[3, 0, j + 1])
        dia[j] = upper + eye * sh[0, j, 0:1, :]
        dia[nc + j] = lower + eye * sh[1, j, 0:1, :]

    count = 2 * nc
    lane = lax.broadcasted_iota(jnp.int32, (1, PANEL, B), 2)
    row = lax.broadcasted_iota(jnp.int32, (1, PANEL, B), 1)
    big_lane = lax.broadcasted_iota(jnp.int32, (B, B), 1)
    big_row = lax.broadcasted_iota(jnp.int32, (B, B), 0)

    def parts(value):
        high = value.astype(BF16).astype(F32)
        rest = value - high
        mid = rest.astype(BF16).astype(F32)
        return high, mid, rest - mid

    def sweep(step, carry):
        first = pl.multiple_of(step * PANEL, PANEL)
        panel = dia[:, pl.ds(first, PANEL), :]
        across = jnp.where(lane < first, -panel, panel)
        inside = (lane >= first) & (lane < first + PANEL)
        across = jnp.where(inside, jnp.where(lane == row + first, -1.0, 0.0), across)
        flat = pltpu.roll(panel.reshape(count * PANEL, B), lax.rem(B - first, B), 1)
        turned = flat.reshape(count, PANEL, B)
        for j in range(0, PANEL, 2):
            e = j + 1
            a = turned[:, j:e, j:e]
            b = turned[:, j:e, e:e + 1]
            c = turned[:, e:e + 1, e:e + 1]
            inv = 1.0 / (a * c - b * b)
            pair = (lane == j) | (lane == e)
            row_j = jnp.where(pair, jnp.where(lane == j, 1.0, 0.0), turned[:, j:e, :])
            row_e = jnp.where(pair, jnp.where(lane == e, 1.0, 0.0), turned[:, e:e + 1, :])
            line_j = (c * row_j - b * row_e) * inv
            line_e = (a * row_e - b * row_j) * inv
            rest = jnp.where(pair, 0.0, turned) - turned[:, :, j:e] * line_j - turned[:, :, e:e + 1] * line_e
            turned = jnp.where(row == j, line_j, jnp.where(row == e, line_e, rest))
        solved = pltpu.roll(turned.reshape(count * PANEL, B), first, 1).reshape(count, PANEL, B)
        hidden = ((big_lane >= first) & (big_lane < first + PANEL)) | (
            (big_row >= first) & (big_row < first + PANEL))
        for m in range(count):
            ah, am, al = parts(across[m])
            bh, bm, bl = parts(solved[m])
            lhs = jnp.concatenate([ah, ah, ah, am, am, al], axis=0).astype(BF16)
            rhs = jnp.concatenate([bh, bm, bl, bh, bm, bh], axis=0).astype(BF16)
            product = lax.dot_general(lhs, rhs, (((0,), (0,)), ((), ())), preferred_element_type=F32)
            dia[m] = jnp.where(hidden, 0.0, dia[m]) - product
        return carry

    lax.fori_loop(0, B // PANEL, sweep, 0)
    inverses = [(remote(dia.at[x * nc + nc - 1], mrim.at[0, x], m_sem.at[x], right), True) for x in range(2)]
    inverses += [(remote(dia.at[x * nc], mrim.at[1, x], m_sem.at[2 + x], left), False) for x in range(2)]
    start_edges(inverses)
    for m in range(count):
        keep(im + m, dia[m])
    wait_edges(inverses)
    ir = im + count
    for side in range(2):
        for x in range(2):
            keep(ir + 2 * side + x, mrim[side, x])

    def times(value, i):
        high, mid, low = split3(value)
        stacked = jnp.concatenate([
            jnp.concatenate([high, high], axis=1),
            jnp.concatenate([mid, mid], axis=1),
            jnp.concatenate([low, low], axis=1)], axis=0)
        out = jnp.dot(stacked, wa[i], preferred_element_type=F32)
        tail = jnp.dot(high, wb[i], preferred_element_type=F32)
        return out[0:nr] + (out[nr:2 * nr] + (out[2 * nr:3 * nr] + tail))

    xs[...] = jnp.zeros_like(xs)
    ps[...] = jnp.zeros_like(ps)
    ss[...] = jnp.zeros_like(ss)
    srim[...] = jnp.zeros_like(srim)
    vlane = lax.broadcasted_iota(jnp.int32, (nr, B), 1)
    vrow = lax.broadcasted_iota(jnp.int32, (nr, B), 0)

    def iterate(t, carry):
        gamma_old, alpha_old = carry
        z = [[times(rs[x, j], im + x * nc + j) for j in range(nc)] for x in range(2)]
        from_left = [times(rrim[0, x], ir + x) for x in range(2)]
        from_right = [times(rrim[1, x], ir + 2 + x) for x in range(2)]
        w = [[z[x][j] * sh[x, j, 0:1, :] for j in range(nc)] for x in range(2)]
        for j in range(nc):
            w[1][j] = w[1][j] + times(z[1][j], il + j)
            flux = times(z[0][j] - z[1][j], i0 + j)
            w[0][j] = w[0][j] + flux
            w[1][j] = w[1][j] - flux
            if j + 1 < nc:
                for x in range(2):
                    flux = times(z[x][j] - z[x][j + 1], i1 + x * nc + j)
                    w[x][j] = w[x][j] + flux
                    w[x][j + 1] = w[x][j + 1] - flux
                flux = times(z[0][j] - z[1][j + 1], i2 + j)
                w[0][j] = w[0][j] + flux
                w[1][j + 1] = w[1][j + 1] - flux
            if j > 0:
                flux = times(z[0][j] - z[1][j - 1], i3 + j)
                w[0][j] = w[0][j] + flux
                w[1][j - 1] = w[1][j - 1] - flux

        e = nc - 1
        for x in range(2):
            w[x][e] = w[x][e] + times(z[x][e] - from_right[x], i1 + x * nc + e)
            w[x][0] = w[x][0] - times(from_left[x] - z[x][0], ih + x)
        w[0][e] = w[0][e] + times(z[0][e] - from_right[1], i2 + e)
        w[1][0] = w[1][0] - times(from_left[0] - z[1][0], ih + 2)
        w[0][0] = w[0][0] + times(z[0][0] - from_left[1], i3)
        w[1][e] = w[1][e] - times(from_right[0] - z[1][e], ih + 3)

        for x in range(2):
            ws[t, 0, x] = w[x][0]
            ws[t, 1, x] = w[x][e]
        rims = [
            (remote(ws.at[t, 0], hv.at[t, 1], v_sem.at[t, 0], left), False),
            (remote(ws.at[t, 1], hv.at[t, 0], v_sem.at[t, 1], right), True),
        ]
        start_edges(rims)

        dot_rz = jnp.zeros((nr, B), F32)
        dot_wz = jnp.zeros((nr, B), F32)
        for x in range(2):
            for j in range(nc):
                dot_rz = dot_rz + rs[x, j] * z[x][j]
                dot_wz = dot_wz + w[x][j] * z[x][j]
        mine = jnp.where(vlane == vrow, jnp.sum(dot_rz, axis=1, keepdims=True), 0.0)
        mine = mine + jnp.where(vlane == vrow + nr, jnp.sum(dot_wz, axis=1, keepdims=True), 0.0)
        packed = mine[0:8]
        for q in range(8, nr, 8):
            packed = packed + mine[q:q + 8]
        red[t, p] = packed
        sends = [remote(red.at[t, p], red.at[t, p], red_sem.at[t, q], peer) for q, peer in enumerate(peers)]
        for copy in sends:
            copy.start()
        for copy in sends:
            copy.wait()
        wait_edges(rims)
        total = red[t, 0]
        for q in range(1, n):
            total = total + red[t, q]
        total = jnp.concatenate([total] * (nr // 8), axis=0)
        gamma = jnp.sum(jnp.where(vlane == vrow, total, 0.0), axis=1, keepdims=True)
        delta = jnp.sum(jnp.where(vlane == vrow + nr, total, 0.0), axis=1, keepdims=True)
        start = t == 0
        ratio = jnp.where(start, 0.0, gamma / gamma_old)
        alpha = gamma / jnp.where(start, delta, delta - ratio * gamma / alpha_old)
        for x in range(2):
            for j in range(nc):
                direction = z[x][j] + ratio * ps[x, j]
                along = w[x][j] + ratio * ss[x, j]
                ps[x, j] = direction
                ss[x, j] = along
                xs[x, j] = xs[x, j] + alpha * direction
                rs[x, j] = rs[x, j] - alpha * along
        for side in range(2):
            for x in range(2):
                along = hv[t, side, x] + ratio * srim[side, x]
                srim[side, x] = along
                rrim[side, x] = rrim[side, x] - alpha * along
        return gamma, alpha

    one = jnp.ones((nr, 1), F32)
    lax.fori_loop(0, ITERS, iterate, (one, one))

    homes = [
        remote(xs.at[other], ret.at[0], ret_sem.at[0], partner),
        remote(rs.at[other], ret.at[1], ret_sem.at[1], partner),
    ]
    for copy in homes:
        copy.start()
    for j in range(nc):
        x_out[0, g * nc + j] = xs[g, j]
        r_out[0, g * nc + j] = rs[g, j]
    for copy in homes:
        copy.wait()
    for j in range(nc):
        x_out[0, other * nc + j] = ret[0, j]
        r_out[0, other * nc + j] = ret[1, j]


def paired_rows(gy_count):
    def run(load, factors, links, shift):
        nc = load.shape[1] // 2
        nr = load.shape[2]
        n = 2 * gy_count
        blocks = 6 * nc + 4 + 2 * nc + 4
        dma = pltpu.SemaphoreType.DMA
        vmem = pltpu.VMEM
        node = (2, nc, nr, B)
        return pl.pallas_call(
            functools.partial(fused, gy_count),
            out_shape=[jax.ShapeDtypeStruct(load.shape, F32)] * 2,
            in_specs=[
                pl.BlockSpec(memory_space=vmem),
                pl.BlockSpec(memory_space=vmem),
                pl.BlockSpec(memory_space=pltpu.SMEM),
                pl.BlockSpec(memory_space=vmem),
            ],
            out_specs=[pl.BlockSpec(memory_space=vmem)] * 2,
            scratch_shapes=[
                vmem((4, 2, nc, B, B), BF16),
                vmem((4, nc, B, B), BF16),
                vmem((4, B, B), BF16),
                vmem((2, nc, 8, B), F32),
                vmem((nc, 8, B), F32),
                vmem((4, 2, nc, B, B), F32),
                vmem((2 * nc, B, B), F32),
                vmem((blocks, 2 * B, B), BF16),
                vmem((blocks, B, B), BF16),
                vmem(node, F32),
                vmem(node, F32),
                vmem(node, F32),
                vmem(node, F32),
                vmem((ITERS, 2, 2, nr, B), F32),
                vmem((ITERS, 2, 2, nr, B), F32),
                vmem((2, 2, B, B), F32),
                vmem((2, 2, nr, B), F32),
                vmem((2, 2, nr, B), F32),
                vmem((ITERS, n, 8, B), F32),
                vmem((2, nc, nr, B), F32),
                dma((4, 2)),
                dma((2, 2)),
                dma((4, 2)),
                dma((4, 2)),
                dma((2, 2)),
                dma((ITERS, 2, 2)),
                dma((ITERS, n - 1, 2)),
                dma((2, 2)),
            ],
            compiler_params=pltpu.CompilerParams(
                collective_id=0, has_side_effects=True, vmem_limit_bytes=48 * 1024 * 1024),
        )(load, factors, links, shift)

    return run


def solution(mesh):
    placed = (
        P(("case", "gx"), "gy", None, None),
        P(None, ("case", "gx"), "gy", None, None),
        P(None, ("case", "gx"), "gy"),
        P(("case", "gx"), "gy", None),
    )
    paired_grid = mesh.shape["gx"] == 2
    return jax.shard_map(
        paired_rows(mesh.shape["gy"]) if paired_grid else local,
        mesh=mesh,
        in_specs=placed,
        out_specs=(P(("case", "gx"), "gy", None, None), P(("case", "gx"), "gy", None, None)),
        check_vma=False,
    )
```

```python
import functools

import jax
import jax.numpy as jnp
from jax import lax
from jax.experimental import pallas as pl
from jax.experimental.pallas import tpu as pltpu
from jax.sharding import PartitionSpec as P

B = 128
ITERS = 8


OFFSETS = ((1, 0), (0, 1), (1, 1), (1, -1))
PRECISE = lax.Precision.HIGHEST


def extended(cells, sides, width):
    for axis, dim in sides:
        count = lax.axis_size(axis)
        ends = count - 1
        head = lax.slice_in_dim(cells, 0, width, axis=dim)
        tail = lax.slice_in_dim(cells, cells.shape[dim] - width, cells.shape[dim], axis=dim)
        cells = jnp.concatenate(
            [
                lax.ppermute(tail, axis, [(i, (i + 1) % count) for i in range(ends)]),
                cells,
                lax.ppermute(head, axis, [((i + 1) % count, i) for i in range(ends)]),
            ],
            axis=dim,
        )
    return cells


def window(padded, step_x, step_y, count_x, count_y):
    return padded[1 + step_x : 1 + step_x + count_x, 1 + step_y : 1 + step_y + count_y]


def inner(left, right):
    return jnp.sum(left * right, axis=(0, 1, 3))


def spread(values):
    return values[None, None, :, None]


def local(load, factors, links, shift):
    count_x, count_y = (load.shape[0], load.shape[1])
    masked = factors * links.astype(jnp.bfloat16)[:, :, :, None, None]
    springs = (
        jnp.einsum("dxyak,dxybk->dxyab", masked, masked, preferred_element_type=jnp.float32) / B
    )
    padded_springs = extended(springs, (("gx", 1), ("gy", 2)), 1)
    forward = padded_springs[:, 1:-1, 1:-1]
    backward = jnp.stack(
        [
            window(
                padded_springs[offset], -OFFSETS[offset][0], -OFFSETS[offset][1], count_x, count_y
            )
            for offset in range(4)
        ]
    )
    identity = jnp.eye(B, dtype=jnp.float32)
    diagonal = shift[..., None] * identity + jnp.sum(forward, axis=0) + jnp.sum(backward, axis=0)
    lower = jnp.linalg.cholesky(diagonal.reshape(-1, B, B))
    inverse = jax.vmap(lambda factor: jax.scipy.linalg.cho_solve((factor, True), identity))(
        lower
    ).reshape(diagonal.shape)
    blocks = jnp.concatenate([diagonal[None], -forward, -backward], axis=0)

    def operate(field):
        padded = extended(field, (("gx", 0), ("gy", 1)), 1)
        pieces = [field]
        pieces = pieces + [
            window(padded, step_x, step_y, count_x, count_y) for step_x, step_y in OFFSETS
        ]
        pieces = pieces + [
            window(padded, -step_x, -step_y, count_x, count_y) for step_x, step_y in OFFSETS
        ]
        return jnp.einsum(
            "kxyab,kxyrb->xyra",
            blocks,
            jnp.stack(pieces),
            precision=PRECISE,
            preferred_element_type=jnp.float32,
        )

    def precondition(field):
        return jnp.einsum(
            "xyab,xyrb->xyra", inverse, field, precision=PRECISE, preferred_element_type=jnp.float32
        )

    def paired(residual, precon, image):
        return lax.psum((inner(residual, precon), inner(image, precon)), ("gx", "gy"))

    solution = jnp.zeros_like(load)
    residual = load
    precon = precondition(residual)
    image = operate(precon)
    gamma, delta = paired(residual, precon, image)
    alpha = gamma / delta
    direction, along = (precon, image)
    for iteration in range(ITERS):
        solution = solution + spread(alpha) * direction
        residual = residual - spread(alpha) * along
        if iteration + 1 < ITERS:
            precon = precondition(residual)
            image = operate(precon)
            gamma_next, delta = paired(residual, precon, image)
            ratio = gamma_next / gamma
            alpha = gamma_next / (delta - ratio * gamma_next / alpha)
            direction = precon + spread(ratio) * direction
            along = image + spread(ratio) * along
            gamma = gamma_next
    return (solution, residual)


F32 = jnp.float32
BF16 = jnp.bfloat16
PANEL = 8


def split3(value):
    high = value.astype(BF16)
    rest = value - high.astype(F32)
    mid = rest.astype(BF16)
    low = (rest - mid.astype(F32)).astype(BF16)
    return high, mid, low


def fused(gy_count, load_ref, fac_ref, links_ref, shift_ref, x_out, r_out,
          fac, out_fac, hal_fac, sh, out_sh, spr, dia, wa, wb,
          xs, rs, ps, ss, us, ws, qs, ys, zs, hv, red, ret,
          fac_sem, half_sem, hal_sem, v_sem, red_sem, ret_sem):
    g = lax.axis_index("gx")
    k = lax.axis_index("gy")
    n = 2 * gy_count
    p = 2 * k + g
    nc = fac.shape[2]
    nr = load_ref.shape[2]
    other = 1 - g
    mesh_id = pl.DeviceIdType.MESH

    def at(gx, gy):
        return {"gx": gx, "gy": gy}

    partner = at(other, k)
    left = at(other, k - other)
    right = at(other, k + g)

    barrier = pltpu.get_barrier_semaphore()
    peers = []
    for q in range(1, n):
        t = lax.rem(p + q, n)
        peers.append(at(lax.rem(t, 2), t // 2))
    for peer in peers:
        pl.semaphore_signal(barrier, inc=1, device_id=peer, device_id_type=mesh_id)

    def remote(src, dst, sems, peer):
        return pltpu.make_async_remote_copy(
            src_ref=src, dst_ref=dst, send_sem=sems.at[0], recv_sem=sems.at[1],
            device_id=peer, device_id_type=mesh_id)

    def start_edges(copies):
        @pl.when(p < n - 1)
        def _():
            for copy, rightward in copies:
                if rightward:
                    copy.start()

        @pl.when(p > 0)
        def _():
            for copy, rightward in copies:
                if not rightward:
                    copy.start()

    def wait_edges(copies):
        @pl.when(p < n - 1)
        def _():
            for copy, rightward in copies:
                if rightward:
                    copy.wait_send()
                else:
                    copy.wait_recv()

        @pl.when(p > 0)
        def _():
            for copy, rightward in copies:
                if rightward:
                    copy.wait_recv()
                else:
                    copy.wait_send()

    for j in range(nc):
        out_sh[j] = jnp.broadcast_to(shift_ref[0, pl.ds(other * nc + j, 1), :], (8, B))
        sh[g, j] = jnp.broadcast_to(shift_ref[0, pl.ds(g * nc + j, 1), :], (8, B))
        for d in range(4):
            here, there = g * nc + j, other * nc + j
            out_fac[d, j] = (fac_ref[d, 0, there].astype(F32) * links_ref[d, 0, there].astype(F32)).astype(BF16)
            fac[d, g, j] = (fac_ref[d, 0, here].astype(F32) * links_ref[d, 0, here].astype(F32)).astype(BF16)
        rs[g, j] = load_ref[0, g * nc + j]

    @pl.when(p == 0)
    def _():
        hal_fac[0:3] = jnp.zeros((3, B, B), BF16)
        hv[:, 0] = jnp.zeros(hv.shape[:1] + hv.shape[2:], F32)

    @pl.when(p == n - 1)
    def _():
        hal_fac[3] = jnp.zeros((B, B), BF16)
        hv[:, 1] = jnp.zeros(hv.shape[:1] + hv.shape[2:], F32)

    pl.semaphore_wait(barrier, n - 1)

    halves = [remote(out_fac.at[d], fac.at[d, g], fac_sem.at[d], partner) for d in (1, 2, 3, 0)]
    halves.append(remote(out_sh, sh.at[g], half_sem.at[0], partner))
    halves.append(remote(load_ref.at[0, pl.ds(other * nc, nc)], rs.at[g], half_sem.at[1], partner))
    for copy in halves:
        copy.start()

    def spring(f):
        return lax.dot_general(f, f, (((1,), (1,)), ((), ())), preferred_element_type=F32) * (1.0 / B)

    for d in range(4):
        for j in range(nc):
            spr[d, g, j] = spring(fac[d, g, j])
    for copy in halves:
        copy.wait()

    sides = [
        (remote(fac.at[1, 0, nc - 1], hal_fac.at[0], hal_sem.at[0], right), True),
        (remote(fac.at[1, 1, nc - 1], hal_fac.at[1], hal_sem.at[1], right), True),
        (remote(fac.at[2, 0, nc - 1], hal_fac.at[2], hal_sem.at[2], right), True),
        (remote(fac.at[3, 0, 0], hal_fac.at[3], hal_sem.at[3], left), False),
    ]

    start_edges(sides)

    for d in range(4):
        for j in range(nc):
            spr[d, other, j] = spring(fac[d, other, j])

    wait_edges(sides)

    def keep(i, value):
        high, mid, low = split3(value)
        wa[i, 0:B] = high
        wa[i, B:2 * B] = mid
        wb[i] = low

    i0, i1, i2, i3, il = 0, nc, 3 * nc, 4 * nc, 5 * nc
    ih = 6 * nc
    im = ih + 4
    for s in range(4):
        keep(ih + s, spring(hal_fac[s]))
    back = [spring(hal_fac[s]) for s in range(4)]
    eye = (lax.broadcasted_iota(jnp.int32, (B, B), 0) == lax.broadcasted_iota(jnp.int32, (B, B), 1)).astype(F32)
    for j in range(nc):
        keep(i0 + j, spr[0, 0, j])
        keep(i1 + j, spr[1, 0, j])
        keep(i1 + nc + j, spr[1, 1, j])
        keep(i2 + j, spr[2, 0, j])
        keep(i3 + j, spr[3, 0, j])
        edge = spr[0, 1, j] + spr[2, 1, j] + spr[3, 1, j]
        keep(il + j, edge)
        before0 = back[0] if j == 0 else spr[1, 0, j - 1]
        before1 = back[1] if j == 0 else spr[1, 1, j - 1]
        upper = spr[0, 0, j] + spr[1, 0, j] + spr[2, 0, j] + spr[3, 0, j] + before0
        lower = edge + spr[1, 1, j] + before1 + spr[0, 0, j]
        lower = lower + (back[2] if j == 0 else spr[2, 0, j - 1])
        lower = lower + (back[3] if j == nc - 1 else spr[3, 0, j + 1])
        dia[j] = upper + eye * sh[0, j, 0:1, :]
        dia[nc + j] = lower + eye * sh[1, j, 0:1, :]

    count = 2 * nc
    lane = lax.broadcasted_iota(jnp.int32, (1, PANEL, B), 2)
    row = lax.broadcasted_iota(jnp.int32, (1, PANEL, B), 1)
    big_lane = lax.broadcasted_iota(jnp.int32, (B, B), 1)
    big_row = lax.broadcasted_iota(jnp.int32, (B, B), 0)

    def parts(value):
        high = value.astype(BF16).astype(F32)
        rest = value - high
        mid = rest.astype(BF16).astype(F32)
        return high, mid, rest - mid

    def sweep(step, carry):
        first = pl.multiple_of(step * PANEL, PANEL)
        panel = dia[:, pl.ds(first, PANEL), :]
        across = jnp.where(lane < first, -panel, panel)
        inside = (lane >= first) & (lane < first + PANEL)
        across = jnp.where(inside, jnp.where(lane == row + first, -1.0, 0.0), across)
        flat = pltpu.roll(panel.reshape(count * PANEL, B), lax.rem(B - first, B), 1)
        turned = flat.reshape(count, PANEL, B)
        for j in range(0, PANEL, 2):
            e = j + 1
            a = turned[:, j:e, j:e]
            b = turned[:, j:e, e:e + 1]
            c = turned[:, e:e + 1, e:e + 1]
            inv = 1.0 / (a * c - b * b)
            pair = (lane == j) | (lane == e)
            row_j = jnp.where(pair, jnp.where(lane == j, 1.0, 0.0), turned[:, j:e, :])
            row_e = jnp.where(pair, jnp.where(lane == e, 1.0, 0.0), turned[:, e:e + 1, :])
            line_j = (c * row_j - b * row_e) * inv
            line_e = (a * row_e - b * row_j) * inv
            rest = jnp.where(pair, 0.0, turned) - turned[:, :, j:e] * line_j - turned[:, :, e:e + 1] * line_e
            turned = jnp.where(row == j, line_j, jnp.where(row == e, line_e, rest))
        solved = pltpu.roll(turned.reshape(count * PANEL, B), first, 1).reshape(count, PANEL, B)
        hidden = ((big_lane >= first) & (big_lane < first + PANEL)) | (
            (big_row >= first) & (big_row < first + PANEL))
        for m in range(count):
            ah, am, al = parts(across[m])
            bh, bm, bl = parts(solved[m])
            lhs = jnp.concatenate([ah, ah, ah, am, am, al], axis=0).astype(BF16)
            rhs = jnp.concatenate([bh, bm, bl, bh, bm, bh], axis=0).astype(BF16)
            product = lax.dot_general(lhs, rhs, (((0,), (0,)), ((), ())), preferred_element_type=F32)
            dia[m] = jnp.where(hidden, 0.0, dia[m]) - product
        return carry

    lax.fori_loop(0, B // PANEL, sweep, 0)
    for m in range(count):
        keep(im + m, dia[m])

    def times(value, i):
        high, mid, low = split3(value)
        stacked = jnp.concatenate([
            jnp.concatenate([high, high], axis=1),
            jnp.concatenate([mid, mid], axis=1),
            jnp.concatenate([low, low], axis=1)], axis=0)
        out = jnp.dot(stacked, wa[i], preferred_element_type=F32)
        tail = jnp.dot(high, wb[i], preferred_element_type=F32)
        return out[0:nr] + (out[nr:2 * nr] + (out[2 * nr:3 * nr] + tail))

    vlane = lax.broadcasted_iota(jnp.int32, (nr, B), 1)
    vrow = lax.broadcasted_iota(jnp.int32, (nr, B), 0)
    e = nc - 1
    nodes = [(x, j) for x in range(2) for j in range(nc)]

    def precondition(field, slot):
        out = [[None] * nc for _ in range(2)]
        for x in range(2):
            for j in sorted({0, e}):
                out[x][j] = times(field[x, j], im + x * nc + j)
            zs[slot, 0, x] = out[x][0]
            zs[slot, 1, x] = out[x][e]
        rims = [
            (remote(zs.at[slot, 0], hv.at[slot, 1], v_sem.at[slot, 0], left), False),
            (remote(zs.at[slot, 1], hv.at[slot, 0], v_sem.at[slot, 1], right), True),
        ]
        start_edges(rims)
        for x in range(2):
            for j in range(1, e):
                out[x][j] = times(field[x, j], im + x * nc + j)
        return out, rims

    def operate(z, rims, slot):
        w = [[z[x][j] * sh[x, j, 0:1, :] for j in range(nc)] for x in range(2)]
        for j in range(nc):
            w[1][j] = w[1][j] + times(z[1][j], il + j)
            flux = times(z[0][j] - z[1][j], i0 + j)
            w[0][j] = w[0][j] + flux
            w[1][j] = w[1][j] - flux
            if j + 1 < nc:
                for x in range(2):
                    flux = times(z[x][j] - z[x][j + 1], i1 + x * nc + j)
                    w[x][j] = w[x][j] + flux
                    w[x][j + 1] = w[x][j + 1] - flux
                flux = times(z[0][j] - z[1][j + 1], i2 + j)
                w[0][j] = w[0][j] + flux
                w[1][j + 1] = w[1][j + 1] - flux
            if j > 0:
                flux = times(z[0][j] - z[1][j - 1], i3 + j)
                w[0][j] = w[0][j] + flux
                w[1][j - 1] = w[1][j - 1] - flux
        wait_edges(rims)
        from_left = [hv[slot, 0, x] for x in range(2)]
        from_right = [hv[slot, 1, x] for x in range(2)]
        for x in range(2):
            w[x][e] = w[x][e] + times(z[x][e] - from_right[x], i1 + x * nc + e)
            w[x][0] = w[x][0] - times(from_left[x] - z[x][0], ih + x)
        w[0][e] = w[0][e] + times(z[0][e] - from_right[1], i2 + e)
        w[1][0] = w[1][0] - times(from_left[0] - z[1][0], ih + 2)
        w[0][0] = w[0][0] + times(z[0][0] - from_left[1], i3)
        w[1][e] = w[1][e] - times(from_right[0] - z[1][e], ih + 3)
        return w

    def send_dots(t):
        dot_rz = jnp.zeros((nr, B), F32)
        dot_wz = jnp.zeros((nr, B), F32)
        for x, j in nodes:
            dot_rz = dot_rz + rs[x, j] * us[x, j]
            dot_wz = dot_wz + ws[x, j] * us[x, j]
        mine = jnp.where(vlane == vrow, jnp.sum(dot_rz, axis=1, keepdims=True), 0.0)
        mine = mine + jnp.where(vlane == vrow + nr, jnp.sum(dot_wz, axis=1, keepdims=True), 0.0)
        packed = mine[0:8]
        for q in range(8, nr, 8):
            packed = packed + mine[q:q + 8]
        red[t, p] = packed
        sends = [remote(red.at[t, p], red.at[t, p], red_sem.at[t, q], peer) for q, peer in enumerate(peers)]
        for copy in sends:
            copy.start()
        return sends

    def receive_dots(t, sends, gamma_old, alpha_old):
        for copy in sends:
            copy.wait()
        total = red[t, 0]
        for q in range(1, n):
            total = total + red[t, q]
        total = jnp.concatenate([total] * (nr // 8), axis=0)
        gamma = jnp.sum(jnp.where(vlane == vrow, total, 0.0), axis=1, keepdims=True)
        delta = jnp.sum(jnp.where(vlane == vrow + nr, total, 0.0), axis=1, keepdims=True)
        start = t == 0
        ratio = jnp.where(start, 0.0, gamma / gamma_old)
        alpha = gamma / jnp.where(start, delta, delta - ratio * gamma / alpha_old)
        return gamma, ratio, alpha

    def advance(ratio, alpha):
        for x, j in nodes:
            direction = us[x, j] + ratio * ps[x, j]
            along = ws[x, j] + ratio * ss[x, j]
            ps[x, j] = direction
            ss[x, j] = along
            xs[x, j] = xs[x, j] + alpha * direction
            rs[x, j] = rs[x, j] - alpha * along

    for state in (xs, ps, ss, qs, ys):
        state[...] = jnp.zeros_like(state)
    first_z, first_rims = precondition(rs, 0)
    first_w = operate(first_z, first_rims, 0)
    for x, j in nodes:
        us[x, j] = first_z[x][j]
        ws[x, j] = first_w[x][j]

    def iterate(t, carry):
        sends = send_dots(t)
        m, rims = precondition(ws, t + 1)
        image = operate(m, rims, t + 1)
        gamma, ratio, alpha = receive_dots(t, sends, *carry)
        advance(ratio, alpha)
        for x, j in nodes:
            q = m[x][j] + ratio * qs[x, j]
            y = image[x][j] + ratio * ys[x, j]
            qs[x, j] = q
            ys[x, j] = y
            us[x, j] = us[x, j] - alpha * q
            ws[x, j] = ws[x, j] - alpha * y
        return gamma, alpha

    one = jnp.ones((nr, 1), F32)
    carry = lax.fori_loop(0, ITERS - 1, iterate, (one, one))
    _, ratio, alpha = receive_dots(ITERS - 1, send_dots(ITERS - 1), *carry)
    advance(ratio, alpha)

    homes = [
        remote(xs.at[other], ret.at[0], ret_sem.at[0], partner),
        remote(rs.at[other], ret.at[1], ret_sem.at[1], partner),
    ]
    for copy in homes:
        copy.start()
    for j in range(nc):
        x_out[0, g * nc + j] = xs[g, j]
        r_out[0, g * nc + j] = rs[g, j]
    for copy in homes:
        copy.wait()
    for j in range(nc):
        x_out[0, other * nc + j] = ret[0, j]
        r_out[0, other * nc + j] = ret[1, j]


def paired_rows(gy_count):
    def run(load, factors, links, shift):
        nc = load.shape[1] // 2
        nr = load.shape[2]
        n = 2 * gy_count
        blocks = 6 * nc + 4 + 2 * nc
        dma = pltpu.SemaphoreType.DMA
        vmem = pltpu.VMEM
        node = (2, nc, nr, B)
        return pl.pallas_call(
            functools.partial(fused, gy_count),
            out_shape=[jax.ShapeDtypeStruct(load.shape, F32)] * 2,
            in_specs=[
                pl.BlockSpec(memory_space=vmem),
                pl.BlockSpec(memory_space=vmem),
                pl.BlockSpec(memory_space=pltpu.SMEM),
                pl.BlockSpec(memory_space=vmem),
            ],
            out_specs=[pl.BlockSpec(memory_space=vmem)] * 2,
            scratch_shapes=[
                vmem((4, 2, nc, B, B), BF16),
                vmem((4, nc, B, B), BF16),
                vmem((4, B, B), BF16),
                vmem((2, nc, 8, B), F32),
                vmem((nc, 8, B), F32),
                vmem((4, 2, nc, B, B), F32),
                vmem((2 * nc, B, B), F32),
                vmem((blocks, 2 * B, B), BF16),
                vmem((blocks, B, B), BF16),
                vmem(node, F32),
                vmem(node, F32),
                vmem(node, F32),
                vmem(node, F32),
                vmem(node, F32),
                vmem(node, F32),
                vmem(node, F32),
                vmem(node, F32),
                vmem((ITERS, 2, 2, nr, B), F32),
                vmem((ITERS, 2, 2, nr, B), F32),
                vmem((ITERS, n, 8, B), F32),
                vmem((2, nc, nr, B), F32),
                dma((4, 2)),
                dma((2, 2)),
                dma((4, 2)),
                dma((ITERS, 2, 2)),
                dma((ITERS, n - 1, 2)),
                dma((2, 2)),
            ],
            compiler_params=pltpu.CompilerParams(
                collective_id=0, has_side_effects=True, vmem_limit_bytes=48 * 1024 * 1024),
        )(load, factors, links, shift)

    return run


def solution(mesh):
    placed = (
        P(("case", "gx"), "gy", None, None),
        P(None, ("case", "gx"), "gy", None, None),
        P(None, ("case", "gx"), "gy"),
        P(("case", "gx"), "gy", None),
    )
    paired_grid = mesh.shape["gx"] == 2
    return jax.shard_map(
        paired_rows(mesh.shape["gy"]) if paired_grid else local,
        mesh=mesh,
        in_specs=placed,
        out_specs=(P(("case", "gx"), "gy", None, None), P(("case", "gx"), "gy", None, None)),
        check_vma=False,
    )
```

```python
import functools

import jax
import jax.numpy as jnp
from jax import lax
from jax.experimental import pallas as pl
from jax.experimental.pallas import tpu as pltpu
from jax.sharding import PartitionSpec as P

B = 128
ITERS = 8


OFFSETS = ((1, 0), (0, 1), (1, 1), (1, -1))
PRECISE = lax.Precision.HIGHEST


def extended(cells, sides, width):
    for axis, dim in sides:
        count = lax.axis_size(axis)
        ends = count - 1
        head = lax.slice_in_dim(cells, 0, width, axis=dim)
        tail = lax.slice_in_dim(cells, cells.shape[dim] - width, cells.shape[dim], axis=dim)
        cells = jnp.concatenate(
            [
                lax.ppermute(tail, axis, [(i, (i + 1) % count) for i in range(ends)]),
                cells,
                lax.ppermute(head, axis, [((i + 1) % count, i) for i in range(ends)]),
            ],
            axis=dim,
        )
    return cells


def window(padded, step_x, step_y, count_x, count_y):
    return padded[1 + step_x : 1 + step_x + count_x, 1 + step_y : 1 + step_y + count_y]


def inner(left, right):
    return jnp.sum(left * right, axis=(0, 1, 3))


def spread(values):
    return values[None, None, :, None]


def local(load, factors, links, shift):
    count_x, count_y = (load.shape[0], load.shape[1])
    masked = factors * links.astype(jnp.bfloat16)[:, :, :, None, None]
    springs = (
        jnp.einsum("dxyak,dxybk->dxyab", masked, masked, preferred_element_type=jnp.float32) / B
    )
    padded_springs = extended(springs, (("gx", 1), ("gy", 2)), 1)
    forward = padded_springs[:, 1:-1, 1:-1]
    backward = jnp.stack(
        [
            window(
                padded_springs[offset], -OFFSETS[offset][0], -OFFSETS[offset][1], count_x, count_y
            )
            for offset in range(4)
        ]
    )
    identity = jnp.eye(B, dtype=jnp.float32)
    diagonal = shift[..., None] * identity + jnp.sum(forward, axis=0) + jnp.sum(backward, axis=0)
    lower = jnp.linalg.cholesky(diagonal.reshape(-1, B, B))
    inverse = jax.vmap(lambda factor: jax.scipy.linalg.cho_solve((factor, True), identity))(
        lower
    ).reshape(diagonal.shape)
    blocks = jnp.concatenate([diagonal[None], -forward, -backward], axis=0)

    def operate(field):
        padded = extended(field, (("gx", 0), ("gy", 1)), 1)
        pieces = [field]
        pieces = pieces + [
            window(padded, step_x, step_y, count_x, count_y) for step_x, step_y in OFFSETS
        ]
        pieces = pieces + [
            window(padded, -step_x, -step_y, count_x, count_y) for step_x, step_y in OFFSETS
        ]
        return jnp.einsum(
            "kxyab,kxyrb->xyra",
            blocks,
            jnp.stack(pieces),
            precision=PRECISE,
            preferred_element_type=jnp.float32,
        )

    def precondition(field):
        return jnp.einsum(
            "xyab,xyrb->xyra", inverse, field, precision=PRECISE, preferred_element_type=jnp.float32
        )

    def paired(residual, precon, image):
        return lax.psum((inner(residual, precon), inner(image, precon)), ("gx", "gy"))

    solution = jnp.zeros_like(load)
    residual = load
    precon = precondition(residual)
    image = operate(precon)
    gamma, delta = paired(residual, precon, image)
    alpha = gamma / delta
    direction, along = (precon, image)
    for iteration in range(ITERS):
        solution = solution + spread(alpha) * direction
        residual = residual - spread(alpha) * along
        if iteration + 1 < ITERS:
            precon = precondition(residual)
            image = operate(precon)
            gamma_next, delta = paired(residual, precon, image)
            ratio = gamma_next / gamma
            alpha = gamma_next / (delta - ratio * gamma_next / alpha)
            direction = precon + spread(ratio) * direction
            along = image + spread(ratio) * along
            gamma = gamma_next
    return (solution, residual)


F32 = jnp.float32
BF16 = jnp.bfloat16
PANEL = 8


def split3(value):
    high = value.astype(BF16)
    rest = value - high.astype(F32)
    mid = rest.astype(BF16)
    low = (rest - mid.astype(F32)).astype(BF16)
    return high, mid, low


def fused(gy_count, load_ref, fac_ref, links_ref, shift_ref, x_out, r_out,
          fac, out_fac, hal_fac, sh, out_sh, spr, dia, wa, wb,
          xs, rs, ps, ss, us, ws, qs, ys, zs, hv, red, ret,
          fac_sem, half_sem, hal_sem, v_sem, red_sem, ret_sem):
    g = lax.axis_index("gx")
    k = lax.axis_index("gy")
    n = 2 * gy_count
    h = lax.rem(g + k, 2)
    p = 2 * k + h
    far = 1 - h
    nc = fac.shape[2]
    nr = load_ref.shape[2]
    other = 1 - g
    mesh_id = pl.DeviceIdType.MESH

    def at(gx, gy):
        return {"gx": gx, "gy": gy}

    partner = at(other, k)
    left = at(lax.rem(g + h, 2), k - far)
    right = at(lax.rem(g + far, 2), k + h)

    barrier = pltpu.get_barrier_semaphore()
    peers = []
    for q in range(1, n):
        t = lax.rem(p + q, n)
        peers.append(at(lax.rem(t + t // 2, 2), t // 2))
    for peer in peers:
        pl.semaphore_signal(barrier, inc=1, device_id=peer, device_id_type=mesh_id)

    def remote(src, dst, sems, peer):
        return pltpu.make_async_remote_copy(
            src_ref=src, dst_ref=dst, send_sem=sems.at[0], recv_sem=sems.at[1],
            device_id=peer, device_id_type=mesh_id)

    def start_edges(copies):
        @pl.when(p < n - 1)
        def _():
            for copy, rightward in copies:
                if rightward:
                    copy.start()

        @pl.when(p > 0)
        def _():
            for copy, rightward in copies:
                if not rightward:
                    copy.start()

    def wait_edges(copies):
        @pl.when(p < n - 1)
        def _():
            for copy, rightward in copies:
                if rightward:
                    copy.wait_send()
                else:
                    copy.wait_recv()

        @pl.when(p > 0)
        def _():
            for copy, rightward in copies:
                if rightward:
                    copy.wait_recv()
                else:
                    copy.wait_send()

    for j in range(nc):
        out_sh[j] = jnp.broadcast_to(shift_ref[0, pl.ds(far * nc + j, 1), :], (8, B))
        sh[g, j] = jnp.broadcast_to(shift_ref[0, pl.ds(h * nc + j, 1), :], (8, B))
        for d in range(4):
            here, there = h * nc + j, far * nc + j
            out_fac[d, j] = (fac_ref[d, 0, there].astype(F32) * links_ref[d, 0, there].astype(F32)).astype(BF16)
            fac[d, g, j] = (fac_ref[d, 0, here].astype(F32) * links_ref[d, 0, here].astype(F32)).astype(BF16)
        rs[g, j] = load_ref[0, h * nc + j]

    @pl.when(p == 0)
    def _():
        hal_fac[0:3] = jnp.zeros((3, B, B), BF16)
        hv[:, 0] = jnp.zeros(hv.shape[:1] + hv.shape[2:], F32)

    @pl.when(p == n - 1)
    def _():
        hal_fac[3] = jnp.zeros((B, B), BF16)
        hv[:, 1] = jnp.zeros(hv.shape[:1] + hv.shape[2:], F32)

    pl.semaphore_wait(barrier, n - 1)

    halves = [remote(out_fac.at[d], fac.at[d, g], fac_sem.at[d], partner) for d in (1, 2, 3, 0)]
    halves.append(remote(out_sh, sh.at[g], half_sem.at[0], partner))
    halves.append(remote(load_ref.at[0, pl.ds(far * nc, nc)], rs.at[g], half_sem.at[1], partner))
    for copy in halves:
        copy.start()

    def spring(f):
        return lax.dot_general(f, f, (((1,), (1,)), ((), ())), preferred_element_type=F32) * (1.0 / B)

    for d in range(4):
        for j in range(nc):
            spr[d, g, j] = spring(fac[d, g, j])
    for copy in halves:
        copy.wait()

    sides = [
        (remote(fac.at[1, 0, nc - 1], hal_fac.at[0], hal_sem.at[0], right), True),
        (remote(fac.at[1, 1, nc - 1], hal_fac.at[1], hal_sem.at[1], right), True),
        (remote(fac.at[2, 0, nc - 1], hal_fac.at[2], hal_sem.at[2], right), True),
        (remote(fac.at[3, 0, 0], hal_fac.at[3], hal_sem.at[3], left), False),
    ]

    start_edges(sides)

    for d in range(4):
        for j in range(nc):
            spr[d, other, j] = spring(fac[d, other, j])

    wait_edges(sides)

    def keep(i, value):
        high, mid, low = split3(value)
        wa[i, 0:B] = high
        wa[i, B:2 * B] = mid
        wb[i] = low

    i0, i1, i2, i3, il = 0, nc, 3 * nc, 4 * nc, 5 * nc
    ih = 6 * nc
    im = ih + 4
    for s in range(4):
        keep(ih + s, spring(hal_fac[s]))
    back = [spring(hal_fac[s]) for s in range(4)]
    eye = (lax.broadcasted_iota(jnp.int32, (B, B), 0) == lax.broadcasted_iota(jnp.int32, (B, B), 1)).astype(F32)
    for j in range(nc):
        keep(i0 + j, spr[0, 0, j])
        keep(i1 + j, spr[1, 0, j])
        keep(i1 + nc + j, spr[1, 1, j])
        keep(i2 + j, spr[2, 0, j])
        keep(i3 + j, spr[3, 0, j])
        edge = spr[0, 1, j] + spr[2, 1, j] + spr[3, 1, j]
        keep(il + j, edge)
        before0 = back[0] if j == 0 else spr[1, 0, j - 1]
        before1 = back[1] if j == 0 else spr[1, 1, j - 1]
        upper = spr[0, 0, j] + spr[1, 0, j] + spr[2, 0, j] + spr[3, 0, j] + before0
        lower = edge + spr[1, 1, j] + before1 + spr[0, 0, j]
        lower = lower + (back[2] if j == 0 else spr[2, 0, j - 1])
        lower = lower + (back[3] if j == nc - 1 else spr[3, 0, j + 1])
        dia[j] = upper + eye * sh[0, j, 0:1, :]
        dia[nc + j] = lower + eye * sh[1, j, 0:1, :]

    count = 2 * nc
    lane = lax.broadcasted_iota(jnp.int32, (1, PANEL, B), 2)
    row = lax.broadcasted_iota(jnp.int32, (1, PANEL, B), 1)
    big_lane = lax.broadcasted_iota(jnp.int32, (B, B), 1)
    big_row = lax.broadcasted_iota(jnp.int32, (B, B), 0)

    def parts(value):
        high = value.astype(BF16).astype(F32)
        rest = value - high
        mid = rest.astype(BF16).astype(F32)
        return high, mid, rest - mid

    def sweep(step, carry):
        first = pl.multiple_of(step * PANEL, PANEL)
        panel = dia[:, pl.ds(first, PANEL), :]
        across = jnp.where(lane < first, -panel, panel)
        inside = (lane >= first) & (lane < first + PANEL)
        across = jnp.where(inside, jnp.where(lane == row + first, -1.0, 0.0), across)
        flat = pltpu.roll(panel.reshape(count * PANEL, B), lax.rem(B - first, B), 1)
        turned = flat.reshape(count, PANEL, B)
        for j in range(0, PANEL, 2):
            e = j + 1
            a = turned[:, j:e, j:e]
            b = turned[:, j:e, e:e + 1]
            c = turned[:, e:e + 1, e:e + 1]
            inv = 1.0 / (a * c - b * b)
            pair = (lane == j) | (lane == e)
            row_j = jnp.where(pair, jnp.where(lane == j, 1.0, 0.0), turned[:, j:e, :])
            row_e = jnp.where(pair, jnp.where(lane == e, 1.0, 0.0), turned[:, e:e + 1, :])
            line_j = (c * row_j - b * row_e) * inv
            line_e = (a * row_e - b * row_j) * inv
            rest = jnp.where(pair, 0.0, turned) - turned[:, :, j:e] * line_j - turned[:, :, e:e + 1] * line_e
            turned = jnp.where(row == j, line_j, jnp.where(row == e, line_e, rest))
        solved = pltpu.roll(turned.reshape(count * PANEL, B), first, 1).reshape(count, PANEL, B)
        hidden = ((big_lane >= first) & (big_lane < first + PANEL)) | (
            (big_row >= first) & (big_row < first + PANEL))
        for m in range(count):
            ah, am, al = parts(across[m])
            bh, bm, bl = parts(solved[m])
            lhs = jnp.concatenate([ah, ah, ah, am, am, al], axis=0).astype(BF16)
            rhs = jnp.concatenate([bh, bm, bl, bh, bm, bh], axis=0).astype(BF16)
            product = lax.dot_general(lhs, rhs, (((0,), (0,)), ((), ())), preferred_element_type=F32)
            dia[m] = jnp.where(hidden, 0.0, dia[m]) - product
        return carry

    lax.fori_loop(0, B // PANEL, sweep, 0)
    for m in range(count):
        keep(im + m, dia[m])

    def times(value, i):
        high, mid, low = split3(value)
        stacked = jnp.concatenate([
            jnp.concatenate([high, high], axis=1),
            jnp.concatenate([mid, mid], axis=1),
            jnp.concatenate([low, low], axis=1)], axis=0)
        out = jnp.dot(stacked, wa[i], preferred_element_type=F32)
        tail = jnp.dot(high, wb[i], preferred_element_type=F32)
        return out[0:nr] + (out[nr:2 * nr] + (out[2 * nr:3 * nr] + tail))

    vlane = lax.broadcasted_iota(jnp.int32, (nr, B), 1)
    vrow = lax.broadcasted_iota(jnp.int32, (nr, B), 0)
    e = nc - 1
    nodes = [(x, j) for x in range(2) for j in range(nc)]

    def precondition(field, slot):
        out = [[None] * nc for _ in range(2)]
        for x in range(2):
            for j in sorted({0, e}):
                out[x][j] = times(field[x, j], im + x * nc + j)
            zs[slot, 0, x] = out[x][0]
            zs[slot, 1, x] = out[x][e]
        rims = [
            (remote(zs.at[slot, 0], hv.at[slot, 1], v_sem.at[slot, 0], left), False),
            (remote(zs.at[slot, 1], hv.at[slot, 0], v_sem.at[slot, 1], right), True),
        ]
        start_edges(rims)
        for x in range(2):
            for j in range(1, e):
                out[x][j] = times(field[x, j], im + x * nc + j)
        return out, rims

    def operate(z, rims, slot):
        w = [[z[x][j] * sh[x, j, 0:1, :] for j in range(nc)] for x in range(2)]
        for j in range(nc):
            w[1][j] = w[1][j] + times(z[1][j], il + j)
            flux = times(z[0][j] - z[1][j], i0 + j)
            w[0][j] = w[0][j] + flux
            w[1][j] = w[1][j] - flux
            if j + 1 < nc:
                for x in range(2):
                    flux = times(z[x][j] - z[x][j + 1], i1 + x * nc + j)
                    w[x][j] = w[x][j] + flux
                    w[x][j + 1] = w[x][j + 1] - flux
                flux = times(z[0][j] - z[1][j + 1], i2 + j)
                w[0][j] = w[0][j] + flux
                w[1][j + 1] = w[1][j + 1] - flux
            if j > 0:
                flux = times(z[0][j] - z[1][j - 1], i3 + j)
                w[0][j] = w[0][j] + flux
                w[1][j - 1] = w[1][j - 1] - flux
        wait_edges(rims)
        from_left = [hv[slot, 0, x] for x in range(2)]
        from_right = [hv[slot, 1, x] for x in range(2)]
        for x in range(2):
            w[x][e] = w[x][e] + times(z[x][e] - from_right[x], i1 + x * nc + e)
            w[x][0] = w[x][0] - times(from_left[x] - z[x][0], ih + x)
        w[0][e] = w[0][e] + times(z[0][e] - from_right[1], i2 + e)
        w[1][0] = w[1][0] - times(from_left[0] - z[1][0], ih + 2)
        w[0][0] = w[0][0] + times(z[0][0] - from_left[1], i3)
        w[1][e] = w[1][e] - times(from_right[0] - z[1][e], ih + 3)
        return w

    def send_dots(t):
        dot_rz = jnp.zeros((nr, B), F32)
        dot_wz = jnp.zeros((nr, B), F32)
        for x, j in nodes:
            dot_rz = dot_rz + rs[x, j] * us[x, j]
            dot_wz = dot_wz + ws[x, j] * us[x, j]
        mine = jnp.where(vlane == vrow, jnp.sum(dot_rz, axis=1, keepdims=True), 0.0)
        mine = mine + jnp.where(vlane == vrow + nr, jnp.sum(dot_wz, axis=1, keepdims=True), 0.0)
        packed = mine[0:8]
        for q in range(8, nr, 8):
            packed = packed + mine[q:q + 8]
        red[t, p] = packed
        sends = [remote(red.at[t, p], red.at[t, p], red_sem.at[t, q], peer) for q, peer in enumerate(peers)]
        for copy in sends:
            copy.start()
        return sends

    def receive_dots(t, sends, gamma_old, alpha_old):
        for copy in sends:
            copy.wait()
        total = red[t, 0]
        for q in range(1, n):
            total = total + red[t, q]
        total = jnp.concatenate([total] * (nr // 8), axis=0)
        gamma = jnp.sum(jnp.where(vlane == vrow, total, 0.0), axis=1, keepdims=True)
        delta = jnp.sum(jnp.where(vlane == vrow + nr, total, 0.0), axis=1, keepdims=True)
        start = t == 0
        ratio = jnp.where(start, 0.0, gamma / gamma_old)
        alpha = gamma / jnp.where(start, delta, delta - ratio * gamma / alpha_old)
        return gamma, ratio, alpha

    def advance(ratio, alpha):
        for x, j in nodes:
            direction = us[x, j] + ratio * ps[x, j]
            along = ws[x, j] + ratio * ss[x, j]
            ps[x, j] = direction
            ss[x, j] = along
            xs[x, j] = xs[x, j] + alpha * direction
            rs[x, j] = rs[x, j] - alpha * along

    for state in (xs, ps, ss, qs, ys):
        state[...] = jnp.zeros_like(state)
    first_z, first_rims = precondition(rs, 0)
    first_w = operate(first_z, first_rims, 0)
    for x, j in nodes:
        us[x, j] = first_z[x][j]
        ws[x, j] = first_w[x][j]

    def iterate(t, carry):
        sends = send_dots(t)
        m, rims = precondition(ws, t + 1)
        image = operate(m, rims, t + 1)
        gamma, ratio, alpha = receive_dots(t, sends, *carry)
        advance(ratio, alpha)
        for x, j in nodes:
            q = m[x][j] + ratio * qs[x, j]
            y = image[x][j] + ratio * ys[x, j]
            qs[x, j] = q
            ys[x, j] = y
            us[x, j] = us[x, j] - alpha * q
            ws[x, j] = ws[x, j] - alpha * y
        return gamma, alpha

    one = jnp.ones((nr, 1), F32)
    carry = lax.fori_loop(0, ITERS - 1, iterate, (one, one))
    _, ratio, alpha = receive_dots(ITERS - 1, send_dots(ITERS - 1), *carry)
    advance(ratio, alpha)

    homes = [
        remote(xs.at[other], ret.at[0], ret_sem.at[0], partner),
        remote(rs.at[other], ret.at[1], ret_sem.at[1], partner),
    ]
    for copy in homes:
        copy.start()
    for j in range(nc):
        x_out[0, h * nc + j] = xs[g, j]
        r_out[0, h * nc + j] = rs[g, j]
    for copy in homes:
        copy.wait()
    for j in range(nc):
        x_out[0, far * nc + j] = ret[0, j]
        r_out[0, far * nc + j] = ret[1, j]


def paired_rows(gy_count):
    def run(load, factors, links, shift):
        nc = load.shape[1] // 2
        nr = load.shape[2]
        n = 2 * gy_count
        blocks = 6 * nc + 4 + 2 * nc
        dma = pltpu.SemaphoreType.DMA
        vmem = pltpu.VMEM
        node = (2, nc, nr, B)
        return pl.pallas_call(
            functools.partial(fused, gy_count),
            out_shape=[jax.ShapeDtypeStruct(load.shape, F32)] * 2,
            in_specs=[
                pl.BlockSpec(memory_space=vmem),
                pl.BlockSpec(memory_space=vmem),
                pl.BlockSpec(memory_space=pltpu.SMEM),
                pl.BlockSpec(memory_space=vmem),
            ],
            out_specs=[pl.BlockSpec(memory_space=vmem)] * 2,
            scratch_shapes=[
                vmem((4, 2, nc, B, B), BF16),
                vmem((4, nc, B, B), BF16),
                vmem((4, B, B), BF16),
                vmem((2, nc, 8, B), F32),
                vmem((nc, 8, B), F32),
                vmem((4, 2, nc, B, B), F32),
                vmem((2 * nc, B, B), F32),
                vmem((blocks, 2 * B, B), BF16),
                vmem((blocks, B, B), BF16),
                vmem(node, F32),
                vmem(node, F32),
                vmem(node, F32),
                vmem(node, F32),
                vmem(node, F32),
                vmem(node, F32),
                vmem(node, F32),
                vmem(node, F32),
                vmem((ITERS, 2, 2, nr, B), F32),
                vmem((ITERS, 2, 2, nr, B), F32),
                vmem((ITERS, n, 8, B), F32),
                vmem((2, nc, nr, B), F32),
                dma((4, 2)),
                dma((2, 2)),
                dma((4, 2)),
                dma((ITERS, 2, 2)),
                dma((ITERS, n - 1, 2)),
                dma((2, 2)),
            ],
            compiler_params=pltpu.CompilerParams(
                collective_id=0, has_side_effects=True, vmem_limit_bytes=48 * 1024 * 1024),
        )(load, factors, links, shift)

    return run


def solution(mesh):
    placed = (
        P(("case", "gx"), "gy", None, None),
        P(None, ("case", "gx"), "gy", None, None),
        P(None, ("case", "gx"), "gy"),
        P(("case", "gx"), "gy", None),
    )
    paired_grid = mesh.shape["gx"] == 2
    return jax.shard_map(
        paired_rows(mesh.shape["gy"]) if paired_grid else local,
        mesh=mesh,
        in_specs=placed,
        out_specs=(P(("case", "gx"), "gy", None, None), P(("case", "gx"), "gy", None, None)),
        check_vma=False,
    )
```
